32 devices in a mesh: dp: 4 (over y, x), head: 8 (over z, core).
Axes of the slice: x: 2, y: 2, z: 4, core: 2. Of those that a mesh axis runs over, the one named last changes fastest.
Arguments:
- latents: bfloat16 [512, 512], P('dp'), may hold values from -6 to 6
- targets: bfloat16 [512, 32768], P('dp', 'head'), may hold values from -6 to 6
- kv_weight: bfloat16 [512, 32768], P(None, 'head'), may hold values from -0.25 to 0.25
- momentum: float32 [512, 8, 4096], P(None, 'head', 'dp'), may hold values from -120 to 120
Outputs:
- momentum_out: float32 [512, 8, 4096], P(None, 'head', 'dp')
- update: float32 [512, 8, 4096], P(None, 'head', 'dp')
The draws below stay inside these ranges and needn't reach their ends.
All inputs are finite; a program needn't handle non-finite values.
Results may differ from the reference program's by a relative error of at most 0.0003.
The reference program's roundings to bfloat16 on the way (of `residual`) count: a program that leaves them out, or rounds other values in their place, can miss the bound.
Values may be sent and summed in bfloat16 or wider, within the bound.
No kernel may reach another device: no remote copies, remote signals or barrier semaphores. Data moves between devices by JAX's collectives and lax.ppermute only.
A program may use at most 64 MiB of HBM per device.

```python
import math
import jax
import jax.numpy as jnp
from jax import lax

R = 512
C = 32768
ITERS = 2
TOKENS = 512
SUB = 4096
N_HEAD = 8


def draw_momentum(key, part):
    key_base = jax.random.fold_in(key, 11)
    key_cols = jax.random.fold_in(key, 12)
    key_rows = jax.random.fold_in(key, 13)
    position = jnp.arange(C, dtype=jnp.float32) / C
    col_scale = jnp.exp(math.log(3.0) * position + jax.random.uniform(key_cols, (C,), jnp.float32, 0.0, math.log(4.0)))
    row_scale = jnp.exp(jax.random.uniform(key_rows, (R,), jnp.float32, 0.0, math.log(10.0)))
    base = jax.random.truncated_normal(key_base, -4.0, 4.0, (R, C), jnp.float32)
    values = 0.25 * base * row_scale[:, None] * col_scale[None, :]
    return values.reshape(R, N_HEAD, SUB).astype(jnp.float32)


def level_of(rng, dims, split, low, top_value):
    def one(dim, shards_of):
        heights = jax.random.uniform(jax.random.fold_in(jax.random.fold_in(rng, 6), dim), (shards_of,), jnp.float32, low / len(split), top_value / len(split))
        return jnp.repeat(jnp.exp(heights), dims[dim] // shards_of).reshape((-1,) + (1,) * (len(dims) - dim - 1))

    level = one(*split[0])
    for cut in split[1:]:
        level = level * one(*cut)
    return level


def bell_draw(own_key, dims, scale, most, split=(), kind=jnp.bfloat16):
    loudness = level_of(own_key, dims, split, -0.22, 0.18) if split else 1.0
    entries = jax.random.normal(own_key, dims, jnp.float32) * scale * loudness
    return jnp.minimum(jnp.maximum(entries, -most), most).astype(kind)


def setup_inputs(seed: int = 0) -> dict:
    seeds = jax.random.split(jax.random.key(seed), 5)
    return {
        "latents": bell_draw(seeds[0], (TOKENS, R), 1.0, 6.0, ((0, 4),)),
        "targets": bell_draw(seeds[1], (TOKENS, C), 1.0, 6.0, ((0, 4), (1, 8))),
        "kv_weight": bell_draw(seeds[2], (R, C), R ** -0.5, 0.25, ((1, 8),)),
        "momentum": draw_momentum(jax.random.fold_in(seeds[4], 71), 0),
    }


decay_rate = 0.95
linear_coef = 3.4445
square_coef = -4.775
quint_coef = 2.0315
epsilon = 1e-07

def reference(latents, targets, kv_weight, momentum):
    residual = (jnp.dot(latents, kv_weight, preferred_element_type=jnp.float32) - targets.astype(jnp.float32)).astype(jnp.bfloat16)
    gradient = jnp.dot(latents.T, residual, preferred_element_type=jnp.float32) * (1.0 / math.sqrt(TOKENS))
    previous = momentum.reshape(R, C)
    momentum_new = decay_rate * previous + gradient
    nesterov = gradient + decay_rate * momentum_new
    inverse = 1.0 / (jnp.sqrt(jnp.sum(nesterov * nesterov)) + epsilon)
    iterate = nesterov * inverse
    for iteration in range(ITERS):
        gram_matrix = jnp.dot(iterate, iterate.T, precision=lax.Precision.HIGHEST)
        polynomial = square_coef * gram_matrix + quint_coef * jnp.dot(gram_matrix, gram_matrix, precision=lax.Precision.HIGHEST)
        iterate = linear_coef * iterate + jnp.dot(polynomial, iterate, precision=lax.Precision.HIGHEST)
    update = iterate * math.sqrt(C)
    return (momentum_new.reshape(R, N_HEAD, SUB), update.reshape(R, N_HEAD, SUB))
```

```python
import functools
import math

import jax
import jax.numpy as jnp
from jax import lax
from jax.experimental import pallas as pl
from jax.experimental.pallas import tpu as pltpu
from jax.sharding import PartitionSpec as P

LANES = 128

decay_rate = 0.95
linear_coef = 3.4445
square_coef = -4.775
quint_coef = 2.0315
epsilon = 1e-07
iterations = 2


ROWS_BY_ROWS = (((1,), (1,)), ((), ()))


def split(value):
    high = value.astype(jnp.bfloat16)
    low = (value - high.astype(jnp.float32)).astype(jnp.bfloat16)
    return high, low


def dot(left, right, dims=(((1,), (0,)), ((), ()))):
    return lax.dot_general(left, right, dims, preferred_element_type=jnp.float32)


def product(left, right):
    left_high, left_low = split(left)
    right_high, right_low = split(right)
    return (
        dot(left_high, right_low) + dot(left_low, right_high) + dot(left_high, right_high)
    )


def swap(value, axis, mask):
    size = lax.axis_size(axis)
    return lax.ppermute(value, axis, [(i, i ^ mask) for i in range(size)])


def pick(stack, index):
    return lax.dynamic_index_in_dim(stack, index, 0, keepdims=False)


def few(size):
    return size in (2, 4)


def scatter_sum(value, axis):
    size = lax.axis_size(axis)
    parts = value.reshape(size, value.shape[0] // size, *value.shape[1:])
    if not few(size):
        return jnp.sum(lax.all_to_all(parts, axis, 0, 0), axis=0)
    me = lax.axis_index(axis)
    arrived = [swap(pick(parts, me ^ mask), axis, mask) for mask in range(1, size)]
    total = pick(parts, me)
    for part in arrived:
        total = total + part
    return total


def gather(value, axis):
    size = lax.axis_size(axis)
    if not few(size):
        return lax.all_gather(value, axis, axis=0, tiled=True)
    me = lax.axis_index(axis)
    parts = jnp.stack([value] + [swap(value, axis, mask) for mask in range(1, size)])
    return jnp.concatenate([pick(parts, me ^ owner) for owner in range(size)], axis=0)


def sum_over_devices(packed):
    heads = lax.axis_size("head")
    core = lax.axis_index("head") % 2
    halves = packed.reshape(2, packed.shape[0] // 2, *packed.shape[1:])
    half = pick(halves, core) + swap(pick(halves, 1 - core), "head", 1)
    part = scatter_sum(half, "dp")
    if heads == 8:
        arrived = [swap(part, "head", 2 * mask) for mask in range(1, 4)]
        part = (part + arrived[0]) + (arrived[1] + arrived[2])
    else:
        mask = 2
        while mask < heads:
            part = part + swap(part, "head", mask)
            mask *= 2
    half = gather(part, "dp")
    other = swap(half, "head", 1)
    return jnp.concatenate(
        [jnp.where(core == 0, half, other), jnp.where(core == 0, other, half)], axis=0
    )


def gram_kernel(blocks, nesterov_ref, packed_ref, high_ref, low_ref):
    high, low = split(nesterov_ref[...])
    high_ref[...] = high
    low_ref[...] = low
    slot = 0
    for i in range(blocks):
        rows = pl.ds(i * LANES, LANES)
        after = pl.ds(i * LANES, (blocks - i) * LANES)
        strip = (
            dot(high_ref[rows, :], low_ref[after, :], ROWS_BY_ROWS)
            + dot(low_ref[rows, :], high_ref[after, :], ROWS_BY_ROWS)
            + dot(high_ref[rows, :], high_ref[after, :], ROWS_BY_ROWS)
        )
        for j in range(blocks - i):
            packed_ref[pl.ds(slot * LANES, LANES), :] = strip[:, j * LANES : (j + 1) * LANES]
            slot += 1


def gram_blocks(nesterov):
    rows, _ = nesterov.shape
    blocks = rows // LANES
    count = blocks * (blocks + 1) // 2
    whole = pl.BlockSpec(memory_space=pltpu.VMEM)
    return pl.pallas_call(
        functools.partial(gram_kernel, blocks),
        out_shape=(
            jax.ShapeDtypeStruct((count * LANES, LANES), jnp.float32),
            jax.ShapeDtypeStruct(nesterov.shape, jnp.bfloat16),
            jax.ShapeDtypeStruct(nesterov.shape, jnp.bfloat16),
        ),
        in_specs=[whole],
        out_specs=(whole, whole, whole),
        name="gram",
    )(nesterov)


def chain_kernel(blocks, scale, packed_ref, high_ref, low_ref, gram_ref):
    slot = 0
    for i in range(blocks):
        for j in range(i, blocks):
            block = packed_ref[pl.ds(slot * LANES, LANES), :]
            gram_ref[pl.ds(i * LANES, LANES), pl.ds(j * LANES, LANES)] = block
            if j > i:
                gram_ref[pl.ds(j * LANES, LANES), pl.ds(i * LANES, LANES)] = block.T
            slot += 1
    gram = gram_ref[...]
    row = lax.broadcasted_iota(jnp.int32, gram.shape, 0)
    column = lax.broadcasted_iota(jnp.int32, gram.shape, 1)
    diagonal = row == column
    squares = jnp.sum(jnp.where(diagonal, gram, 0.0), keepdims=True)
    inverse = 1.0 / (jnp.sqrt(squares) + epsilon)
    gram = (gram * inverse) * inverse
    identity = jnp.where(diagonal, linear_coef, 0.0)
    total = None
    for iteration in range(iterations):
        factor = identity + square_coef * gram + quint_coef * product(gram, gram)
        total = factor if total is None else product(factor, total)
        if iteration + 1 < iterations:
            gram = product(product(gram, factor), factor)
    high, low = split(total * (inverse * scale))
    high_ref[...] = high
    low_ref[...] = low


def chain(packed, rows, scale):
    whole = pl.BlockSpec(memory_space=pltpu.VMEM)
    square = jax.ShapeDtypeStruct((rows, rows), jnp.bfloat16)
    return pl.pallas_call(
        functools.partial(chain_kernel, rows // LANES, scale),
        out_shape=(square, square),
        in_specs=[whole],
        out_specs=(whole, whole),
        scratch_shapes=[pltpu.VMEM((rows, rows), jnp.float32)],
        name="chain",
    )(packed)


def update_kernel(tiles, left_high_ref, left_low_ref, high_ref, low_ref, out_ref):
    left_high = left_high_ref[...]
    result = (
        dot(left_high, low_ref[...])
        + dot(left_low_ref[...], high_ref[...])
        + dot(left_high, high_ref[...])
    )
    for i in range(result.shape[0] // 8):
        for j in range(tiles):
            out_ref[pl.ds(i * 8 * tiles + j, 8, stride=tiles), :] = result[
                i * 8 : (i + 1) * 8, j * LANES : (j + 1) * LANES
            ]


def apply_update(left_high, left_low, high, low):
    rows, columns = high.shape
    tiles = columns // LANES
    block = LANES
    left = pl.BlockSpec((block, rows), lambda i: (i, 0))
    whole = pl.BlockSpec((rows, columns), lambda i: (0, 0))
    return pl.pallas_call(
        functools.partial(update_kernel, tiles),
        out_shape=jax.ShapeDtypeStruct((rows * tiles, LANES), jnp.float32),
        grid=(rows // block,),
        in_specs=[left, left, whole, whole],
        out_specs=pl.BlockSpec((block * tiles, LANES), lambda i: (i, 0)),
        name="update",
    )(left_high, left_low, high, low)


def columns_of(array, index, width):
    return lax.dynamic_slice_in_dim(array, index * width, width, axis=1)


def local(total_columns, latents, targets, kv_weight, momentum):
    rows = momentum.shape[0]
    width = momentum.shape[2]
    groups = lax.axis_size("dp")
    tokens = latents.shape[0]
    me = lax.axis_index("dp")
    weight = columns_of(kv_weight, me, width)
    if few(groups):
        inputs = [(latents, columns_of(targets, me, width))]
        for mask in range(1, groups):
            sent = jnp.concatenate([columns_of(targets, me ^ mask, width), latents], axis=1)
            got = swap(sent, "dp", mask)
            inputs.append((got[:, width:], got[:, :width]))
    else:
        inputs = [
            (
                lax.all_gather(latents, "dp", axis=0, tiled=True),
                lax.all_to_all(targets, "dp", split_axis=1, concat_axis=0, tiled=True),
            )
        ]
    gradient = None
    for part, wanted in inputs:
        residual = (dot(part, weight) - wanted.astype(jnp.float32)).astype(jnp.bfloat16)
        term = dot(part, residual, (((0,), (0,)), ((), ())))
        gradient = term if gradient is None else gradient + term
    gradient = gradient * (1.0 / math.sqrt(tokens * groups))
    momentum_new = decay_rate * momentum.reshape(rows, width) + gradient
    nesterov = gradient + decay_rate * momentum_new
    packed, high, low = gram_blocks(nesterov)
    packed = sum_over_devices(packed)
    left_high, left_low = chain(packed, rows, math.sqrt(total_columns))
    update = apply_update(left_high, left_low, high, low)
    return momentum_new.reshape(rows, 1, width), update.reshape(rows, 1, width)


def solution(mesh):
    def step(latents, targets, kv_weight, momentum):
        total_columns = kv_weight.shape[1]
        return jax.shard_map(
            functools.partial(local, total_columns),
            mesh=mesh,
            in_specs=(P("dp", None), P("dp", "head"), P(None, "head"), P(None, "head", "dp")),
            out_specs=(P(None, "head", "dp"), P(None, "head", "dp")),
            check_vma=False,
        )(latents, targets, kv_weight, momentum)

    return step
```

```python
import functools
import math

import jax
import jax.numpy as jnp
from jax import lax
from jax.experimental import pallas as pl
from jax.experimental.pallas import tpu as pltpu
from jax.sharding import PartitionSpec as P

LANES = 128

decay_rate = 0.95
linear_coef = 3.4445
square_coef = -4.775
quint_coef = 2.0315
epsilon = 1e-07
iterations = 2


ROWS_BY_ROWS = (((1,), (1,)), ((), ()))


def split(value):
    high = value.astype(jnp.bfloat16)
    low = (value - high.astype(jnp.float32)).astype(jnp.bfloat16)
    return high, low


def dot(left, right, dims=(((1,), (0,)), ((), ()))):
    return lax.dot_general(left, right, dims, preferred_element_type=jnp.float32)


def product(left, right):
    left_high, left_low = split(left)
    right_high, right_low = split(right)
    return (
        dot(left_high, right_low) + dot(left_low, right_high) + dot(left_high, right_high)
    )


def swap(value, axis, mask):
    size = lax.axis_size(axis)
    return lax.ppermute(value, axis, [(i, i ^ mask) for i in range(size)])


def pick(stack, index):
    return lax.dynamic_index_in_dim(stack, index, 0, keepdims=False)


def few(size):
    return size in (2, 4)


def scatter_sum(value, axis):
    size = lax.axis_size(axis)
    parts = value.reshape(size, value.shape[0] // size, *value.shape[1:])
    if not few(size):
        return jnp.sum(lax.all_to_all(parts, axis, 0, 0), axis=0)
    me = lax.axis_index(axis)
    arrived = [swap(pick(parts, me ^ mask), axis, mask) for mask in range(1, size)]
    total = pick(parts, me)
    for part in arrived:
        total = total + part
    return total


def gather(value, axis):
    size = lax.axis_size(axis)
    if not few(size):
        return lax.all_gather(value, axis, axis=0, tiled=True)
    me = lax.axis_index(axis)
    parts = jnp.stack([value] + [swap(value, axis, mask) for mask in range(1, size)])
    return jnp.concatenate([pick(parts, me ^ owner) for owner in range(size)], axis=0)


def sum_over_devices(packed):
    heads = lax.axis_size("head")
    core = lax.axis_index("head") % 2
    halves = packed.reshape(2, packed.shape[0] // 2, *packed.shape[1:])
    half = pick(halves, core) + swap(pick(halves, 1 - core), "head", 1)
    part = scatter_sum(half, "dp")
    if heads == 8:
        arrived = [swap(part, "head", 2 * mask) for mask in range(1, 4)]
        part = (part + arrived[0]) + (arrived[1] + arrived[2])
    else:
        mask = 2
        while mask < heads:
            part = part + swap(part, "head", mask)
            mask *= 2
    half = gather(part, "dp")
    other = swap(half, "head", 1)
    return jnp.concatenate(
        [jnp.where(core == 0, half, other), jnp.where(core == 0, other, half)], axis=0
    )


def tile_rows(i, j, tiles):
    return pl.ds(i * 8 * tiles + j, 8, stride=tiles)


def front_kernel(arrivals, tiles, scale, *refs):
    (lat_ref, lat_t_ref, weight_ref), refs = refs[:3], refs[3:]
    wanted_refs, refs = refs[:arrivals], refs[arrivals:]
    (targets_ref, momentum_ref, momentum_out_ref, packed_ref), refs = refs[:4], refs[4:]
    high_out_ref, low_out_ref, mine, old, new, residual, nesterov, high_ref, low_ref, sems = refs
    rows, width = nesterov.shape
    load = pltpu.make_async_copy(momentum_ref, old, sems.at[0])
    arrived = sum(wanted_ref.shape[0] for wanted_ref in wanted_refs)
    if arrived < lat_ref.shape[0]:
        first = pl.multiple_of(lax.axis_index("dp") * width, width)
        own = pltpu.make_async_copy(targets_ref.at[:, pl.ds(first, width)], mine, sems.at[1])
        own.start()
        wanted_refs = (*wanted_refs, mine)
    load.start()
    predicted = dot(lat_ref[...], weight_ref[...])
    start = 0
    for wanted_ref in wanted_refs:
        if start == arrived:
            own.wait()
        count = wanted_ref.shape[0]
        residual[pl.ds(start, count), :] = (
            predicted[start : start + count] - wanted_ref[...].astype(jnp.float32)
        ).astype(jnp.bfloat16)
        start += count
    nesterov[...] = dot(lat_t_ref[...], residual[...])
    load.wait()
    for i in range(rows // 8):
        for j in range(tiles):
            here = (pl.ds(i * 8, 8), pl.ds(j * LANES, LANES))
            gradient = nesterov[here] * scale
            fresh = decay_rate * old[tile_rows(i, j, tiles), :] + gradient
            new[tile_rows(i, j, tiles), :] = fresh
            nesterov[here] = gradient + decay_rate * fresh
    high, low = split(nesterov[...])
    high_ref[...] = high
    low_ref[...] = low
    stores = [
        pltpu.make_async_copy(new, momentum_out_ref, sems.at[0]),
        pltpu.make_async_copy(high_ref, high_out_ref, sems.at[1]),
        pltpu.make_async_copy(low_ref, low_out_ref, sems.at[2]),
    ]
    for store in stores:
        store.start()
    blocks = rows // LANES
    slot = 0
    for i in range(blocks):
        strip = pl.ds(i * LANES, LANES)
        after = pl.ds(i * LANES, (blocks - i) * LANES)
        gram = (
            dot(high_ref[strip, :], low_ref[after, :], ROWS_BY_ROWS)
            + dot(low_ref[strip, :], high_ref[after, :], ROWS_BY_ROWS)
            + dot(high_ref[strip, :], high_ref[after, :], ROWS_BY_ROWS)
        )
        for j in range(blocks - i):
            packed_ref[pl.ds(slot * LANES, LANES), :] = gram[:, j * LANES : (j + 1) * LANES]
            slot += 1
    for store in stores:
        store.wait()


def in_hbm(array):
    return pltpu.with_memory_space_constraint(array, pltpu.HBM)


def front(lat, weight, wanted, targets, momentum, scale):
    rows, width = weight.shape
    blocks, tiles = rows // LANES, width // LANES
    count = blocks * (blocks + 1) // 2
    vmem = pl.BlockSpec(memory_space=pltpu.VMEM)
    hbm = pl.BlockSpec(memory_space=pl.ANY)
    half = pltpu.HBM((rows, width), jnp.bfloat16)
    linear = (rows * tiles, LANES)
    return pl.pallas_call(
        functools.partial(front_kernel, len(wanted), tiles, scale),
        out_shape=(
            pltpu.HBM(linear, jnp.float32),
            jax.ShapeDtypeStruct((count * LANES, LANES), jnp.float32),
            half,
            half,
        ),
        in_specs=[vmem] * (3 + len(wanted)) + [hbm, hbm],
        out_specs=(hbm, vmem, hbm, hbm),
        scratch_shapes=[
            pltpu.VMEM((targets.shape[0], width), targets.dtype),
            pltpu.VMEM(linear, jnp.float32),
            pltpu.VMEM(linear, jnp.float32),
            pltpu.VMEM((lat.shape[0], width), jnp.bfloat16),
            pltpu.VMEM((rows, width), jnp.float32),
            pltpu.VMEM((rows, width), jnp.bfloat16),
            pltpu.VMEM((rows, width), jnp.bfloat16),
            pltpu.SemaphoreType.DMA((3,)),
        ],
        compiler_params=pltpu.CompilerParams(vmem_limit_bytes=28 << 20),
        name="front",
    )(lat, lat.T, weight, *wanted, in_hbm(targets), in_hbm(momentum.reshape(linear)))


def finish_kernel(
    tiles, scale, packed_ref, high_hbm, low_hbm, out_hbm, gram_ref, high_ref, low_ref, result, out, sems
):
    loads = [
        pltpu.make_async_copy(high_hbm, high_ref, sems.at[0]),
        pltpu.make_async_copy(low_hbm, low_ref, sems.at[1]),
    ]
    for load in loads:
        load.start()
    rows = gram_ref.shape[0]
    blocks = rows // LANES
    slot = 0
    for i in range(blocks):
        for j in range(i, blocks):
            block = packed_ref[pl.ds(slot * LANES, LANES), :]
            gram_ref[pl.ds(i * LANES, LANES), pl.ds(j * LANES, LANES)] = block
            if j > i:
                gram_ref[pl.ds(j * LANES, LANES), pl.ds(i * LANES, LANES)] = block.T
            slot += 1
    gram = gram_ref[...]
    row = lax.broadcasted_iota(jnp.int32, gram.shape, 0)
    column = lax.broadcasted_iota(jnp.int32, gram.shape, 1)
    diagonal = row == column
    squares = jnp.sum(jnp.where(diagonal, gram, 0.0), keepdims=True)
    inverse = 1.0 / (jnp.sqrt(squares) + epsilon)
    gram = (gram * inverse) * inverse
    identity = jnp.where(diagonal, linear_coef, 0.0)
    total = None
    for iteration in range(iterations):
        factor = identity + square_coef * gram + quint_coef * product(gram, gram)
        total = factor if total is None else product(factor, total)
        if iteration + 1 < iterations:
            gram = product(product(gram, factor), factor)
    left_high, left_low = split(total * (inverse * scale))
    for load in loads:
        load.wait()
    step = rows // 2
    stores = []
    for part in range(2):
        here = slice(part * step, (part + 1) * step)
        result[...] = (
            dot(left_high[here], low_ref[...])
            + dot(left_low[here], high_ref[...])
            + dot(left_high[here], high_ref[...])
        )
        for i in range(step // 8):
            for j in range(tiles):
                out[tile_rows(part * step // 8 + i, j, tiles), :] = result[
                    pl.ds(i * 8, 8), pl.ds(j * LANES, LANES)
                ]
        chunk = pl.ds(part * step * tiles, step * tiles)
        store = pltpu.make_async_copy(out.at[chunk, :], out_hbm.at[chunk, :], sems.at[2 + part])
        store.start()
        stores.append(store)
    for store in stores:
        store.wait()


def finish(packed, high, low, scale):
    rows, width = high.shape
    tiles = width // LANES
    linear = (rows * tiles, LANES)
    vmem = pl.BlockSpec(memory_space=pltpu.VMEM)
    hbm = pl.BlockSpec(memory_space=pl.ANY)
    return pl.pallas_call(
        functools.partial(finish_kernel, tiles, scale),
        out_shape=pltpu.HBM(linear, jnp.float32),
        in_specs=[vmem, hbm, hbm],
        out_specs=hbm,
        scratch_shapes=[
            pltpu.VMEM((rows, rows), jnp.float32),
            pltpu.VMEM((rows, width), jnp.bfloat16),
            pltpu.VMEM((rows, width), jnp.bfloat16),
            pltpu.VMEM((rows // 2, width), jnp.float32),
            pltpu.VMEM(linear, jnp.float32),
            pltpu.SemaphoreType.DMA((4,)),
        ],
        compiler_params=pltpu.CompilerParams(vmem_limit_bytes=28 << 20),
        name="finish",
    )(packed, in_hbm(high), in_hbm(low))


def columns_of(array, index, width):
    return lax.dynamic_slice_in_dim(array, index * width, width, axis=1)


def gather_tokens(latents, targets, width):
    groups = lax.axis_size("dp")
    if not few(groups):
        lat = lax.all_gather(latents, "dp", axis=0, tiled=True)
        wanted = lax.all_to_all(targets, "dp", split_axis=1, concat_axis=0, tiled=True)
        return lat, [wanted]
    me = lax.axis_index("dp")
    core = lax.axis_index("head") % 2
    tokens, rows = latents.shape
    mine = pick(latents.reshape(2, tokens // 2, rows), core)
    wanted = [columns_of(targets, me ^ mask, width) for mask in range(1, groups)]
    mine, *wanted = lax.optimization_barrier((mine, *wanted))
    first = jnp.stack([swap(mine, "dp", mask) for mask in range(1, groups)])
    second = swap(first, "head", 1)
    others = jnp.stack(
        [jnp.where(core == 0, first, second), jnp.where(core == 0, second, first)], axis=1
    )
    lat = jnp.concatenate([others.reshape((groups - 1) * tokens, rows), latents], axis=0)
    wanted = [swap(wanted[mask - 1], "dp", mask) for mask in range(1, groups)]
    return lat, wanted


def local(total_columns, latents, targets, kv_weight, momentum):
    rows = momentum.shape[0]
    width = momentum.shape[2]
    weight = columns_of(kv_weight, lax.axis_index("dp"), width)
    lat, wanted = gather_tokens(latents, targets, width)
    momentum_new, packed, high, low = front(
        lat, weight, wanted, targets, momentum, 1.0 / math.sqrt(lat.shape[0])
    )
    packed = sum_over_devices(packed)
    update = finish(packed, high, low, math.sqrt(total_columns))
    return momentum_new.reshape(rows, 1, width), update.reshape(rows, 1, width)


def solution(mesh):
    def step(latents, targets, kv_weight, momentum):
        total_columns = kv_weight.shape[1]
        return jax.shard_map(
            functools.partial(local, total_columns),
            mesh=mesh,
            in_specs=(P("dp", None), P("dp", "head"), P(None, "head"), P(None, "head", "dp")),
            out_specs=(P(None, "head", "dp"), P(None, "head", "dp")),
            check_vma=False,
        )(latents, targets, kv_weight, momentum)

    return step
```

```python
import functools
import math

import jax
import jax.numpy as jnp
from jax import lax
from jax.experimental import pallas as pl
from jax.experimental.pallas import tpu as pltpu
from jax.sharding import PartitionSpec as P


LANES = 128

decay_rate = 0.95
linear_coef = 3.4445
square_coef = -4.775
quint_coef = 2.0315
epsilon = 1e-07
iterations = 2


ROWS_BY_ROWS = (((1,), (1,)), ((), ()))


def split(value):
    high = value.astype(jnp.bfloat16)
    low = (value - high.astype(jnp.float32)).astype(jnp.bfloat16)
    return high, low


def dot(left, right, dims=(((1,), (0,)), ((), ()))):
    return lax.dot_general(left, right, dims, preferred_element_type=jnp.float32)


def product(left, right):
    left_high, left_low = split(left)
    right_high, right_low = split(right)
    return (
        dot(left_high, right_low) + dot(left_low, right_high) + dot(left_high, right_high)
    )


def swap(value, axis, mask):
    size = lax.axis_size(axis)
    return lax.ppermute(value, axis, [(i, i ^ mask) for i in range(size)])


def pick(stack, index):
    return lax.dynamic_index_in_dim(stack, index, 0, keepdims=False)


def few(size):
    return size in (2, 4)


def scatter_sum(value, axis):
    size = lax.axis_size(axis)
    parts = value.reshape(size, value.shape[0] // size, *value.shape[1:])
    if not few(size):
        return jnp.sum(lax.all_to_all(parts, axis, 0, 0), axis=0)
    me = lax.axis_index(axis)
    arrived = [swap(pick(parts, me ^ mask), axis, mask) for mask in range(1, size)]
    total = pick(parts, me)
    for part in arrived:
        total = total + part
    return total


def gather(value, axis):
    size = lax.axis_size(axis)
    if not few(size):
        return lax.all_gather(value, axis, axis=0, tiled=True)
    me = lax.axis_index(axis)
    parts = jnp.stack([value] + [swap(value, axis, mask) for mask in range(1, size)])
    return jnp.concatenate([pick(parts, me ^ owner) for owner in range(size)], axis=0)


def sum_over_devices(packed):
    heads = lax.axis_size("head")
    core = lax.axis_index("head") % 2
    halves = packed.reshape(2, packed.shape[0] // 2, *packed.shape[1:])
    half = pick(halves, core) + swap(pick(halves, 1 - core), "head", 1)
    part = scatter_sum(half, "dp")
    if heads == 8:
        arrived = [swap(part, "head", 2 * mask) for mask in range(1, 4)]
        part = (part + arrived[0]) + (arrived[1] + arrived[2])
    else:
        mask = 2
        while mask < heads:
            part = part + swap(part, "head", mask)
            mask *= 2
    half = gather(part, "dp")
    other = swap(half, "head", 1)
    return jnp.concatenate(
        [jnp.where(core == 0, half, other), jnp.where(core == 0, other, half)], axis=0
    )


def tile_rows(i, j, tiles):
    return pl.ds(i * 8 * tiles + j, 8, stride=tiles)


def front_kernel(arrivals, tiles, scale, *refs):
    (lat_ref, lat_t_ref, weight_ref), refs = refs[:3], refs[3:]
    wanted_refs, refs = refs[:arrivals], refs[arrivals:]
    (targets_ref, momentum_ref, momentum_out_ref, packed_ref), refs = refs[:4], refs[4:]
    high_out_ref, low_out_ref, mine, old, new, residual, nesterov, high_ref, low_ref, sems = refs
    rows, width = nesterov.shape
    load = pltpu.make_async_copy(momentum_ref, old, sems.at[0])
    arrived = sum(wanted_ref.shape[0] for wanted_ref in wanted_refs)
    if arrived < lat_ref.shape[0]:
        first = pl.multiple_of(lax.axis_index("dp") * width, width)
        own = pltpu.make_async_copy(targets_ref.at[:, pl.ds(first, width)], mine, sems.at[1])
        own.start()
        wanted_refs = (*wanted_refs, mine)
    load.start()
    predicted = dot(lat_ref[...], weight_ref[...])
    start = 0
    for wanted_ref in wanted_refs:
        if start == arrived:
            own.wait()
        count = wanted_ref.shape[0]
        residual[pl.ds(start, count), :] = (
            predicted[start : start + count] - wanted_ref[...].astype(jnp.float32)
        ).astype(jnp.bfloat16)
        start += count
    nesterov[...] = dot(lat_t_ref[...], residual[...])
    load.wait()
    for i in range(rows // 8):
        for j in range(tiles):
            here = (pl.ds(i * 8, 8), pl.ds(j * LANES, LANES))
            gradient = nesterov[here] * scale
            fresh = decay_rate * old[tile_rows(i, j, tiles), :] + gradient
            new[tile_rows(i, j, tiles), :] = fresh
            nesterov[here] = gradient + decay_rate * fresh
    high, low = split(nesterov[...])
    high_ref[...] = high
    low_ref[...] = low
    stores = [
        pltpu.make_async_copy(new, momentum_out_ref, sems.at[0]),
        pltpu.make_async_copy(high_ref, high_out_ref, sems.at[1]),
        pltpu.make_async_copy(low_ref, low_out_ref, sems.at[2]),
    ]
    for store in stores:
        store.start()
    blocks = rows // LANES
    slot = 0
    for i in range(blocks):
        strip = pl.ds(i * LANES, LANES)
        after = pl.ds(i * LANES, (blocks - i) * LANES)
        gram = (
            dot(high_ref[strip, :], low_ref[after, :], ROWS_BY_ROWS)
            + dot(low_ref[strip, :], high_ref[after, :], ROWS_BY_ROWS)
            + dot(high_ref[strip, :], high_ref[after, :], ROWS_BY_ROWS)
        )
        for j in range(blocks - i):
            packed_ref[pl.ds(slot * LANES, LANES), :] = gram[:, j * LANES : (j + 1) * LANES]
            slot += 1
    for store in stores:
        store.wait()


def in_hbm(array):
    return pltpu.with_memory_space_constraint(array, pltpu.HBM)


def front(lat, weight, wanted, targets, momentum, scale):
    rows, width = weight.shape
    blocks, tiles = rows // LANES, width // LANES
    count = blocks * (blocks + 1) // 2
    vmem = pl.BlockSpec(memory_space=pltpu.VMEM)
    hbm = pl.BlockSpec(memory_space=pl.ANY)
    half = pltpu.HBM((rows, width), jnp.bfloat16)
    linear = (rows * tiles, LANES)
    return pl.pallas_call(
        functools.partial(front_kernel, len(wanted), tiles, scale),
        out_shape=(
            pltpu.HBM(linear, jnp.float32),
            jax.ShapeDtypeStruct((count * LANES, LANES), jnp.float32),
            half,
            half,
        ),
        in_specs=[vmem] * (3 + len(wanted)) + [hbm, hbm],
        out_specs=(hbm, vmem, hbm, hbm),
        scratch_shapes=[
            pltpu.VMEM((targets.shape[0], width), targets.dtype),
            pltpu.VMEM(linear, jnp.float32),
            pltpu.VMEM(linear, jnp.float32),
            pltpu.VMEM((lat.shape[0], width), jnp.bfloat16),
            pltpu.VMEM((rows, width), jnp.float32),
            pltpu.VMEM((rows, width), jnp.bfloat16),
            pltpu.VMEM((rows, width), jnp.bfloat16),
            pltpu.SemaphoreType.DMA((3,)),
        ],
        compiler_params=pltpu.CompilerParams(vmem_limit_bytes=28 << 20),
        name="front",
    )(lat, lat.T, weight, *wanted, in_hbm(targets), in_hbm(momentum.reshape(linear)))


def finish_kernel(
    tiles, scale, packed_ref, high_hbm, low_hbm, out_hbm, gram_ref, high_ref, low_ref, result, out, sems
):
    loads = [
        pltpu.make_async_copy(high_hbm, high_ref, sems.at[0]),
        pltpu.make_async_copy(low_hbm, low_ref, sems.at[1]),
    ]
    for load in loads:
        load.start()
    rows = gram_ref.shape[0]
    blocks = rows // LANES
    slot = 0
    for i in range(blocks):
        for j in range(i, blocks):
            block = packed_ref[pl.ds(slot * LANES, LANES), :]
            gram_ref[pl.ds(i * LANES, LANES), pl.ds(j * LANES, LANES)] = block
            if j > i:
                gram_ref[pl.ds(j * LANES, LANES), pl.ds(i * LANES, LANES)] = block.T
            slot += 1
    gram = gram_ref[...]
    row = lax.broadcasted_iota(jnp.int32, gram.shape, 0)
    column = lax.broadcasted_iota(jnp.int32, gram.shape, 1)
    diagonal = row == column
    squares = jnp.sum(jnp.where(diagonal, gram, 0.0), keepdims=True)
    inverse = 1.0 / (jnp.sqrt(squares) + epsilon)
    gram = (gram * inverse) * inverse
    identity = jnp.where(diagonal, linear_coef, 0.0)
    total = None
    for iteration in range(iterations):
        factor = identity + square_coef * gram + quint_coef * product(gram, gram)
        total = factor if total is None else product(factor, total)
        if iteration + 1 < iterations:
            gram = product(product(gram, factor), factor)
    left_high, left_low = split(total * (inverse * scale))
    for load in loads:
        load.wait()
    step = rows // 2
    stores = []
    for part in range(2):
        here = slice(part * step, (part + 1) * step)
        result[...] = (
            dot(left_high[here], low_ref[...])
            + dot(left_low[here], high_ref[...])
            + dot(left_high[here], high_ref[...])
        )
        for i in range(step // 8):
            for j in range(tiles):
                out[tile_rows(part * step // 8 + i, j, tiles), :] = result[
                    pl.ds(i * 8, 8), pl.ds(j * LANES, LANES)
                ]
        chunk = pl.ds(part * step * tiles, step * tiles)
        store = pltpu.make_async_copy(out.at[chunk, :], out_hbm.at[chunk, :], sems.at[2 + part])
        store.start()
        stores.append(store)
    for store in stores:
        store.wait()


def finish(packed, high, low, scale):
    rows, width = high.shape
    tiles = width // LANES
    linear = (rows * tiles, LANES)
    vmem = pl.BlockSpec(memory_space=pltpu.VMEM)
    hbm = pl.BlockSpec(memory_space=pl.ANY)
    return pl.pallas_call(
        functools.partial(finish_kernel, tiles, scale),
        out_shape=pltpu.HBM(linear, jnp.float32),
        in_specs=[vmem, hbm, hbm],
        out_specs=hbm,
        scratch_shapes=[
            pltpu.VMEM((rows, rows), jnp.float32),
            pltpu.VMEM((rows, width), jnp.bfloat16),
            pltpu.VMEM((rows, width), jnp.bfloat16),
            pltpu.VMEM((rows // 2, width), jnp.float32),
            pltpu.VMEM(linear, jnp.float32),
            pltpu.SemaphoreType.DMA((4,)),
        ],
        compiler_params=pltpu.CompilerParams(vmem_limit_bytes=28 << 20),
        name="finish",
    )(packed, in_hbm(high), in_hbm(low))


def columns_of(array, index, width):
    return lax.dynamic_slice_in_dim(array, index * width, width, axis=1)


def gather_tokens(latents, targets, width):
    groups = lax.axis_size("dp")
    if not few(groups):
        lat = lax.all_gather(latents, "dp", axis=0, tiled=True)
        wanted = lax.all_to_all(targets, "dp", split_axis=1, concat_axis=0, tiled=True)
        return lat, [wanted]
    me = lax.axis_index("dp")
    core = lax.axis_index("head") % 2
    tokens, rows = latents.shape
    mine = pick(latents.reshape(2, tokens // 2, rows), core)
    wanted = [columns_of(targets, me ^ mask, width) for mask in range(1, groups)]
    first = []
    for mask in range(1, groups):
        first.append(swap(mine, "dp", mask))
    first = jnp.stack(first)
    second = swap(first, "head", 1)
    others = jnp.stack(
        [jnp.where(core == 0, first, second), jnp.where(core == 0, second, first)], axis=1
    )
    lat = jnp.concatenate([others.reshape((groups - 1) * tokens, rows), latents], axis=0)
    arrived = []
    for mask in range(1, groups):
        arrived.append(swap(wanted[mask - 1], "dp", mask))
    return lat, arrived


def local(total_columns, latents, targets, kv_weight, momentum):
    rows = momentum.shape[0]
    width = momentum.shape[2]
    weight = columns_of(kv_weight, lax.axis_index("dp"), width)
    lat, wanted = gather_tokens(latents, targets, width)
    momentum_new, packed, high, low = front(
        lat, weight, wanted, targets, momentum, 1.0 / math.sqrt(lat.shape[0])
    )
    packed = sum_over_devices(packed)
    update = finish(packed, high, low, math.sqrt(total_columns))
    return momentum_new.reshape(rows, 1, width), update.reshape(rows, 1, width)


def solution(mesh):

    def step(latents, targets, kv_weight, momentum):
        total_columns = kv_weight.shape[1]
        return jax.shard_map(
            functools.partial(local, total_columns),
            mesh=mesh,
            in_specs=(P("dp", None), P("dp", "head"), P(None, "head"), P(None, "head", "dp")),
            out_specs=(P(None, "head", "dp"), P(None, "head", "dp")),
            check_vma=False,
        )(latents, targets, kv_weight, momentum)

    return step
```

```python
import functools
import math

import jax
import jax.numpy as jnp
from jax import lax
from jax.experimental import pallas as pl
from jax.experimental.pallas import tpu as pltpu
from jax.sharding import PartitionSpec as P


LANES = 128

decay_rate = 0.95
linear_coef = 3.4445
square_coef = -4.775
quint_coef = 2.0315
epsilon = 1e-07
iterations = 2


ROWS_BY_ROWS = (((1,), (1,)), ((), ()))
COLUMNS_BY_ROWS = (((0,), (0,)), ((), ()))


def split(value):
    high = value.astype(jnp.bfloat16)
    low = (value - high.astype(jnp.float32)).astype(jnp.bfloat16)
    return high, low


def dot(left, right, dims=(((1,), (0,)), ((), ()))):
    return lax.dot_general(left, right, dims, preferred_element_type=jnp.float32)


def swap(value, axis, mask):
    size = lax.axis_size(axis)
    return lax.ppermute(value, axis, [(i, i ^ mask) for i in range(size)])


def pick(stack, index):
    return lax.dynamic_index_in_dim(stack, index, 0, keepdims=False)


def few(size):
    return size in (2, 4)


def scatter_sum(value, axis):
    size = lax.axis_size(axis)
    parts = value.reshape(size, value.shape[0] // size, *value.shape[1:])
    if not few(size):
        return jnp.sum(lax.all_to_all(parts, axis, 0, 0), axis=0)
    me = lax.axis_index(axis)
    arrived = [swap(pick(parts, me ^ mask), axis, mask) for mask in range(1, size)]
    total = pick(parts, me)
    for part in arrived:
        total = total + part
    return total


def gather(value, axis):
    size = lax.axis_size(axis)
    if not few(size):
        return lax.all_gather(value, axis, axis=0, tiled=True)
    me = lax.axis_index(axis)
    parts = jnp.stack([value] + [swap(value, axis, mask) for mask in range(1, size)])
    return jnp.concatenate([pick(parts, me ^ owner) for owner in range(size)], axis=0)


def sum_over_devices(packed):
    heads = lax.axis_size("head")
    core = lax.axis_index("head") % 2
    halves = packed.reshape(2, packed.shape[0] // 2, *packed.shape[1:])
    half = pick(halves, core) + swap(pick(halves, 1 - core), "head", 1)
    part = scatter_sum(half, "dp")
    if heads == 8:
        arrived = []
        for mask in range(1, 4):
            arrived.append(swap(part, "head", 2 * mask))
        part = (part + arrived[0]) + (arrived[1] + arrived[2])
    else:
        mask = 2
        while mask < heads:
            part = part + swap(part, "head", mask)
            mask *= 2
    half = gather(part, "dp")
    other = swap(half, "head", 1)
    return jnp.concatenate(
        [jnp.where(core == 0, half, other), jnp.where(core == 0, other, half)], axis=0
    )


def packed_rows(rows, pieces):
    blocks = rows // LANES
    folded = blocks // 2
    used = (blocks * (blocks - 1) // 2 + folded) * LANES + folded
    unit = 8 * pieces
    return -(-used // unit) * unit


def above(blocks):
    return [(i, j) for i in range(blocks) for j in range(i + 1, blocks)]


def block_at(index):
    return pl.ds(index * LANES, LANES)


def positions():
    row = lax.broadcasted_iota(jnp.int32, (LANES, LANES), 0)
    column = lax.broadcasted_iota(jnp.int32, (LANES, LANES), 1)
    return row, column


def pack(block_of, blocks, packed_ref):
    row, column = positions()
    slot = 0
    for i, j in above(blocks):
        packed_ref[block_at(slot), :] = block_of(i, j)
        slot += 1
    diagonals = []
    for i in range(0, blocks, 2):
        second = block_of(i + 1, i + 1)
        packed_ref[block_at(slot), :] = jnp.where(row <= column, block_of(i, i), second)
        diagonals.append(jnp.sum(jnp.where(row == column, second, 0.0), axis=0, keepdims=True))
        slot += 1
    start = slot * LANES
    rest = packed_ref.shape[0] - start
    place = lax.broadcasted_iota(jnp.int32, (rest, LANES), 0)
    tail = jnp.zeros((rest, LANES), jnp.float32)
    for k, diagonal in enumerate(diagonals):
        tail = jnp.where(place == k, diagonal, tail)
    packed_ref[pl.ds(start, rest), :] = tail


def unpack(packed_ref, blocks, square_ref):
    row, column = positions()
    slot = 0
    for i, j in above(blocks):
        block = packed_ref[block_at(slot), :]
        square_ref[block_at(i), block_at(j)] = block
        square_ref[block_at(j), block_at(i)] = block.T
        slot += 1
    start = (slot + blocks // 2) * LANES
    trace = jnp.zeros((1, 1), jnp.float32)
    for i in range(0, blocks, 2):
        block = packed_ref[block_at(slot), :]
        turned = block.T
        diagonal = packed_ref[pl.ds(start + i // 2, 1), :]
        square_ref[block_at(i), block_at(i)] = jnp.where(row <= column, block, turned)
        square_ref[block_at(i + 1), block_at(i + 1)] = jnp.where(
            row > column, block, jnp.where(row < column, turned, diagonal)
        )
        trace = trace + jnp.sum(jnp.where(row == column, block, 0.0), keepdims=True)
        trace = trace + jnp.sum(diagonal, keepdims=True)
        slot += 1
    return trace


def tile_rows(i, j, tiles):
    return pl.ds(i * 8 * tiles + j, 8, stride=tiles)


def momentum_rows(ref, start, j, tiles):
    return jnp.concatenate(
        [ref[pl.ds((start + part) * tiles + j, 8, stride=tiles), :] for part in (0, 8)], axis=0
    )


def front_kernel(arrivals, tiles, scale, *refs):
    (lat_ref, weight_ref), refs = refs[:2], refs[2:]
    wanted_refs, refs = refs[:arrivals], refs[arrivals:]
    (targets_ref, momentum_ref, gradient_ref, packed_ref), refs = refs[:4], refs[4:]
    mine, old, residual, high_ref, low_ref, sems = refs
    rows, width = high_ref.shape
    load = pltpu.make_async_copy(momentum_ref, old, sems.at[0])
    arrived = sum(wanted_ref.shape[0] for wanted_ref in wanted_refs)
    if arrived < lat_ref.shape[0]:
        first = pl.multiple_of(lax.axis_index("dp") * width, width)
        own = pltpu.make_async_copy(targets_ref.at[:, pl.ds(first, width)], mine, sems.at[1])
        own.start()
        wanted_refs = (*wanted_refs, mine)
    load.start()
    start = 0
    for wanted_ref in wanted_refs:
        count = wanted_ref.shape[0]
        here = pl.ds(start, count)
        predicted = dot(lat_ref[here, :], weight_ref[...])
        if start == arrived:
            own.wait()
        residual[here, :] = (predicted - wanted_ref[...].astype(jnp.float32)).astype(jnp.bfloat16)
        start += count
    load.wait()
    for block in range(rows // LANES):
        first = block * LANES
        gradient = dot(lat_ref[:, block_at(block)], residual[...], COLUMNS_BY_ROWS) * scale
        gradient_ref[block_at(block), :] = gradient
        for i in range(0, LANES, 16):
            for j in range(tiles):
                piece = gradient[i : i + 16, j * LANES : (j + 1) * LANES]
                fresh = decay_rate * momentum_rows(old, first + i, j, tiles) + piece
                high, low = split(piece + decay_rate * fresh)
                here = (pl.ds(first + i, 16), block_at(j))
                high_ref[here] = high
                low_ref[here] = low
    half = rows // 2

    def gram(i, j):
        left, right = pl.ds(i * half, half), pl.ds(j * half, half)
        return (
            dot(high_ref[left, :], low_ref[right, :], ROWS_BY_ROWS)
            + dot(low_ref[left, :], high_ref[right, :], ROWS_BY_ROWS)
            + dot(high_ref[left, :], high_ref[right, :], ROWS_BY_ROWS)
        )

    quarters = {(0, 0): gram(0, 0), (0, 1): gram(0, 1), (1, 1): gram(1, 1)}
    per = half // LANES

    def block_of(i, j):
        quarter = quarters[i // per, j // per]
        i, j = i % per, j % per
        return quarter[i * LANES : (i + 1) * LANES, j * LANES : (j + 1) * LANES]

    pack(block_of, rows // LANES, packed_ref)


def in_hbm(array):
    return pltpu.with_memory_space_constraint(array, pltpu.HBM)


def front(lat, weight, wanted, targets, momentum, scale, pieces):
    rows, width = weight.shape
    vmem = pl.BlockSpec(memory_space=pltpu.VMEM)
    hbm = pl.BlockSpec(memory_space=pl.ANY)
    return pl.pallas_call(
        functools.partial(front_kernel, len(wanted), width // LANES, scale),
        out_shape=(
            pltpu.VMEM((rows, width), jnp.float32),
            pltpu.VMEM((packed_rows(rows, pieces), LANES), jnp.float32),
        ),
        in_specs=[vmem] * (2 + len(wanted)) + [hbm, hbm],
        out_specs=(vmem, vmem),
        scratch_shapes=[
            pltpu.VMEM((targets.shape[0], width), targets.dtype),
            pltpu.VMEM(momentum.shape, jnp.float32),
            pltpu.VMEM((lat.shape[0], width), jnp.bfloat16),
            pltpu.VMEM((rows, width), jnp.bfloat16),
            pltpu.VMEM((rows, width), jnp.bfloat16),
            pltpu.SemaphoreType.DMA((2,)),
        ],
        compiler_params=pltpu.CompilerParams(vmem_limit_bytes=24 << 20),
        name="front",
    )(lat, weight, *wanted, in_hbm(targets), in_hbm(momentum))


def momentum_kernel(tiles, gradient_ref, old, new, high_ref, low_ref):
    for i in range(0, gradient_ref.shape[0], 16):
        for j in range(tiles):
            here = (pl.ds(i, 16), block_at(j))
            piece = gradient_ref[here]
            fresh = decay_rate * momentum_rows(old, i, j, tiles) + piece
            for part in (0, 8):
                new[tile_rows((i + part) // 8, j, tiles), :] = fresh[part : part + 8]
            high_ref[here], low_ref[here] = split(piece + decay_rate * fresh)


def momentum_step(gradient, momentum):
    rows, width = gradient.shape
    tiles = width // LANES
    half = pltpu.HBM((rows, width), jnp.bfloat16)
    wide = pl.BlockSpec((LANES, width), lambda i: (i, 0))
    linear = pl.BlockSpec((LANES * tiles, LANES), lambda i: (i, 0))
    return pl.pallas_call(
        functools.partial(momentum_kernel, tiles),
        out_shape=(pltpu.HBM(momentum.shape, jnp.float32), half, half),
        grid=(rows // LANES,),
        in_specs=[wide, linear],
        out_specs=(linear, wide, wide),
        compiler_params=pltpu.CompilerParams(vmem_limit_bytes=16 << 20),
        name="momentum_step",
    )(gradient, in_hbm(momentum))


def symmetric_product(left, right):
    (left_high, left_low), (right_high, right_low) = left, right
    half = left_high.shape[0] // 2

    def part(i, j):
        rows, columns = slice(i * half, (i + 1) * half), slice(j * half, (j + 1) * half)
        return (
            dot(left_high[rows], right_low[:, columns])
            + dot(left_low[rows], right_high[:, columns])
            + dot(left_high[rows], right_high[:, columns])
        )

    corner, side, last = part(0, 0), part(0, 1), part(1, 1)
    return jnp.concatenate(
        [jnp.concatenate([corner, side], axis=1), jnp.concatenate([side.T, last], axis=1)], axis=0
    )


def finish_kernel(
    tiles, scale, packed_ref, high_hbm, low_hbm, out_hbm, square_ref, high_ref, low_ref, out, sems
):
    loads = [
        pltpu.make_async_copy(high_hbm, high_ref, sems.at[0]),
        pltpu.make_async_copy(low_hbm, low_ref, sems.at[1]),
    ]
    for load in loads:
        load.start()
    rows = square_ref.shape[0]
    squares = unpack(packed_ref, rows // LANES, square_ref)
    inverse = 1.0 / (jnp.sqrt(squares) + epsilon)
    gram = (square_ref[...] * inverse) * inverse
    row = lax.broadcasted_iota(jnp.int32, gram.shape, 0)
    column = lax.broadcasted_iota(jnp.int32, gram.shape, 1)
    identity = jnp.where(row == column, linear_coef, 0.0)
    total = None
    for iteration in range(iterations):
        parts = split(gram)
        factor = (
            identity + square_coef * gram + quint_coef * symmetric_product(parts, parts)
        )
        factor_parts = split(factor)
        total = factor if total is None else symmetric_product(split(total), factor_parts)
        if iteration + 1 < iterations:
            once = symmetric_product(parts, factor_parts)
            gram = symmetric_product(split(once), factor_parts)
    left_high, left_low = split(total * (inverse * scale))
    for load in loads:
        load.wait()
    stores = []
    for block in range(rows // LANES):
        here = slice(block * LANES, (block + 1) * LANES)
        result = (
            dot(left_high[here], low_ref[...])
            + dot(left_low[here], high_ref[...])
            + dot(left_high[here], high_ref[...])
        )
        for i in range(LANES // 8):
            for j in range(tiles):
                out[tile_rows(block * LANES // 8 + i, j, tiles), :] = result[
                    i * 8 : (i + 1) * 8, j * LANES : (j + 1) * LANES
                ]
        chunk = pl.ds(block * LANES * tiles, LANES * tiles)
        store = pltpu.make_async_copy(out.at[chunk, :], out_hbm.at[chunk, :], sems.at[2 + block])
        store.start()
        stores.append(store)
    for store in stores:
        store.wait()


def finish(packed, high, low, scale):
    rows, width = high.shape
    tiles = width // LANES
    linear = (rows * tiles, LANES)
    vmem = pl.BlockSpec(memory_space=pltpu.VMEM)
    hbm = pl.BlockSpec(memory_space=pl.ANY)
    return pl.pallas_call(
        functools.partial(finish_kernel, tiles, scale),
        out_shape=pltpu.HBM(linear, jnp.float32),
        in_specs=[vmem, hbm, hbm],
        out_specs=hbm,
        scratch_shapes=[
            pltpu.VMEM((rows, rows), jnp.float32),
            pltpu.VMEM((rows, width), jnp.bfloat16),
            pltpu.VMEM((rows, width), jnp.bfloat16),
            pltpu.VMEM(linear, jnp.float32),
            pltpu.SemaphoreType.DMA((2 + rows // LANES,)),
        ],
        compiler_params=pltpu.CompilerParams(vmem_limit_bytes=28 << 20),
        name="finish",
    )(packed, in_hbm(high), in_hbm(low))


def columns_of(array, index, width):
    return lax.dynamic_slice_in_dim(array, index * width, width, axis=1)


def gather_tokens(latents, targets, width):
    groups = lax.axis_size("dp")
    if not few(groups):
        lat = lax.all_gather(latents, "dp", axis=0, tiled=True)
        wanted = lax.all_to_all(targets, "dp", split_axis=1, concat_axis=0, tiled=True)
        return lat, [wanted]
    me = lax.axis_index("dp")
    core = lax.axis_index("head") % 2
    tokens, rows = latents.shape
    mine = pick(latents.reshape(2, tokens // 2, rows), core)
    wanted = [columns_of(targets, me ^ mask, width) for mask in range(1, groups)]
    first = []
    for mask in range(1, groups):
        first.append(swap(mine, "dp", mask))
    first = jnp.stack(first)
    second = swap(first, "head", 1)
    others = jnp.stack(
        [jnp.where(core == 0, first, second), jnp.where(core == 0, second, first)], axis=1
    )
    lat = jnp.concatenate([others.reshape((groups - 1) * tokens, rows), latents], axis=0)
    arrived = []
    for mask in range(1, groups):
        arrived.append(swap(wanted[mask - 1], "dp", mask))
    return lat, arrived


def local(total_columns, latents, targets, kv_weight, momentum):
    rows = momentum.shape[0]
    width = momentum.shape[2]
    weight = columns_of(kv_weight, lax.axis_index("dp"), width)
    lat, wanted = gather_tokens(latents, targets, width)
    momentum = momentum.reshape(rows * width // LANES, LANES)
    scale = 1.0 / math.sqrt(lat.shape[0])
    gradient, packed = front(lat, weight, wanted, targets, momentum, scale, 2 * lax.axis_size("dp"))
    momentum_new, high, low = momentum_step(gradient, momentum)
    packed = sum_over_devices(packed)
    update = finish(packed, high, low, math.sqrt(total_columns))
    return momentum_new.reshape(rows, 1, width), update.reshape(rows, 1, width)


def solution(mesh):

    def step(latents, targets, kv_weight, momentum):
        total_columns = kv_weight.shape[1]
        return jax.shard_map(
            functools.partial(local, total_columns),
            mesh=mesh,
            in_specs=(P("dp", None), P("dp", "head"), P(None, "head"), P(None, "head", "dp")),
            out_specs=(P(None, "head", "dp"), P(None, "head", "dp")),
            check_vma=False,
        )(latents, targets, kv_weight, momentum)

    return step
```
